32 devices in a mesh: grp: 2 (over y), date: 4 (over x, core), strip: 4 (over z).
Axes of the slice: x: 2, y: 2, z: 4, core: 2. Of those that a mesh axis runs over, the one named last changes fastest.
Arguments:
- acquisitions: bfloat16 [16, 64, 2, 16384], P(('grp', 'date'), 'strip'), parts along dimension 0, may hold values from -22 to 22
- partners: int32 [2, 16], P(None, ('grp', 'date')), parts along dimension 1, may hold values from 0 to 7, as said below
- band_shifts: int32 [2, 16], P(None, ('grp', 'date')), parts along dimension 1, may hold values from -24 to 24
Outputs:
- interferograms: bfloat16 [2, 16, 2, 64, 4096], P(None, ('grp', 'date'), None, 'strip'), parts along dimension 1
- coherence: bfloat16 [2, 16, 64, 4096], P(None, ('grp', 'date'), 'strip'), parts along dimension 1
The draws below stay inside these ranges and needn't reach their ends.
There are 2 independent parts, one for each index of `grp`. The reference program is written for one: setup_inputs(seed, part) draws one part's arguments, and reference() takes and returns one part's arrays. A program takes and returns all parts, laid end to end along the dimension named above; each array names one. Nothing has to cross between parts.
Inputs may be any that keep to these rules, and one draw needn't show every extreme that they name: For each matching m and each date group g (dates g * 2 to (g + 1) * 2 - 1), the partners of the group's dates are the 2 different dates of one other group: g with its lowest bit flipped for m = 0, and (g + 2) modulo 4 for m = 1.
All inputs are finite; a program needn't handle non-finite values.
Results may differ from the reference program's by a relative error of at most 0.0075.
Values may be sent and summed in bfloat16 or wider, within the bound.
A program may use at most 64 MiB of HBM per device.

```python
import math
import jax
import jax.numpy as jnp
from jax import lax

RG = 16384
DATE_DEV = 2
NDATES = 8
AZ = 64


def draw_acquisitions(key, part):
    scene = jnp.clip(jax.random.normal(jax.random.fold_in(key, 11), (AZ, 2, RG), jnp.float32), -5.0, 5.0)
    levels = jax.random.uniform(jax.random.fold_in(key, 12), (NDATES,), jnp.float32, 0.3, 0.9)
    noise = jnp.clip(jax.random.normal(jax.random.fold_in(key, 13), (NDATES, AZ, 2, RG), jnp.float32), -5.0, 5.0)
    mixed = levels[:, None, None, None] * scene[None] + jnp.sqrt(1.0 - levels * levels)[:, None, None, None] * noise
    return mixed.astype(jnp.bfloat16)


def draw_partners(key, part):
    groups = NDATES // DATE_DEV
    scores = jax.random.randint(jax.random.fold_in(key, 21), (2, groups, DATE_DEV), 0, 1 << 20) * DATE_DEV + jnp.arange(DATE_DEV, dtype=jnp.int32)
    slot_order = jnp.argsort(scores, axis=2, stable=True).astype(jnp.int32)
    home = jnp.arange(groups, dtype=jnp.int32)
    nearby = home + 1 - 2 * (home % 2)
    faraway = (home + groups // 2) % groups
    target = jnp.stack([nearby, faraway])
    return (target[:, :, None] * DATE_DEV + slot_order).reshape(2, NDATES)


def place_ends(values, stream_key, low, high):
    longest = values.shape.index(max(values.shape))
    spots = []
    for shift in (0, 1):
        where = [jax.random.randint(jax.random.fold_in(stream_key, axis), (), 0, length) for axis, length in enumerate(values.shape)]
        where[longest] = (where[longest] + shift) % values.shape[longest]
        spots.append(tuple(where))
    return values.at[spots[0]].set(low).at[spots[1]].set(high)


def setup_inputs(seed: int = 0, part: int = 0) -> dict:
    streams_of = jax.random.split(jax.random.key(seed), 4)
    part_splits = jax.random.split(jax.random.fold_in(streams_of[3], part), 4)
    return {
        "acquisitions": draw_acquisitions(jax.random.fold_in(jax.random.fold_in(streams_of[3], part), 71), part),
        "partners": draw_partners(jax.random.fold_in(jax.random.fold_in(streams_of[3], part), 71), part),
        "band_shifts": place_ends(jax.random.randint(part_splits[2], (2, NDATES), -24, 25), jax.random.fold_in(part_splits[2], 1), -24, 24).astype(jnp.int32),
    }


band_width = 0.8
bin_count = 256.0
epsilon = 1e-06

def make_taps(shift_bin):
    positions = jnp.arange(64, dtype=jnp.float32)
    centred = positions - 31.5
    hamming = 0.54 - 0.46 * jnp.cos(2.0 * math.pi * positions / 63.0)
    lowpass = hamming * band_width * jnp.sinc(band_width * centred)
    angles = 2.0 * math.pi * shift_bin.astype(jnp.float32) * centred / bin_count
    return ((lowpass * jnp.cos(angles)).astype(jnp.bfloat16), (lowpass * jnp.sin(angles)).astype(jnp.bfloat16))

def band_filter(image_rows, taps_real, taps_imag):
    signal = image_rows[:, 0, :].astype(jnp.float32) + 1j * image_rows[:, 1, :].astype(jnp.float32)
    padded = jnp.pad(signal, ((0, 0), (32, 31)))
    kernel = (taps_real.astype(jnp.float32) + 1j * taps_imag.astype(jnp.float32))[::-1]
    length = 1 << (RG + 126).bit_length()
    spectrum = jnp.fft.fft(padded, length, axis=1) * jnp.fft.fft(kernel, length)[None, :]
    result = jnp.fft.ifft(spectrum, axis=1)[:, 63:63 + RG]
    return jnp.stack([jnp.real(result), jnp.imag(result)], axis=1).astype(jnp.bfloat16)

def range_looks(values):
    return values.reshape(values.shape[0], values.shape[1] // 4, 4).sum(axis=2)

def look_sums(first_band, second_band):
    first_real = first_band[:, 0].astype(jnp.float32)
    first_imag = first_band[:, 1].astype(jnp.float32)
    second_real = second_band[:, 0].astype(jnp.float32)
    second_imag = second_band[:, 1].astype(jnp.float32)
    return jnp.stack([range_looks(first_real * second_real + first_imag * second_imag), range_looks(first_imag * second_real - first_real * second_imag), range_looks(first_real * first_real + first_imag * first_imag), range_looks(second_real * second_real + second_imag * second_imag)])

def azimuth_window(framed, row_count):
    running = framed[:, 0:row_count]
    for offset in range(1, 20):
        running = running + framed[:, offset:offset + row_count]
    return running

def finish(window):
    mean_cross = (window[0:2] / 80.0).astype(jnp.bfloat16)
    magnitude = jnp.sqrt(window[0] * window[0] + window[1] * window[1])
    coherent = (magnitude / jnp.sqrt(window[2] * window[3] + epsilon)).astype(jnp.bfloat16)
    return (mean_cross, coherent)

def reference(acquisitions, partners, band_shifts):
    date_index = jnp.arange(NDATES, dtype=jnp.int32)
    cross_list = []
    coherence_list = []
    for match_index in range(2):

        def one_pair(pair_entry):
            own_date, other_date, shift_bin = pair_entry
            first_rows = lax.dynamic_index_in_dim(acquisitions, own_date, 0, keepdims=False)
            second_rows = lax.dynamic_index_in_dim(acquisitions, other_date, 0, keepdims=False)
            taps_real, taps_imag = make_taps(shift_bin)
            look_terms = look_sums(band_filter(first_rows, taps_real, taps_imag), band_filter(second_rows, taps_real, taps_imag))
            framed = jnp.pad(look_terms, ((0, 0), (10, 10), (0, 0)))
            return finish(azimuth_window(framed, look_terms.shape[1]))
        mean_cross, coherent = lax.map(one_pair, (date_index, partners[match_index].astype(jnp.int32), band_shifts[match_index]))
        cross_list.append(mean_cross)
        coherence_list.append(coherent)
    return (jnp.stack(cross_list), jnp.stack(coherence_list))
```

```python
import math

import jax
import jax.numpy as jnp
from jax import lax
from jax.experimental import pallas as pl
from jax.experimental.pallas import tpu as pltpu
from jax.sharding import PartitionSpec as P

band_width = 0.8
bin_count = 256.0
epsilon = 1e-06
below = 10
above = 9
lanes = 128
segments = 16


def partner(block, axis, distance):
    count = lax.axis_size(axis)
    route = []
    for low in range(count):
        high = low | 1 << distance
        if high != low and high < count:
            route += [(low, high), (high, low)]
    return lax.ppermute(block, axis, route)


def make_taps(shift_bins):
    positions = jnp.arange(64, dtype=jnp.float32)
    centred = positions - 31.5
    hamming = 0.54 - 0.46 * jnp.cos(2.0 * math.pi * positions / 63.0)
    lowpass = hamming * band_width * jnp.sinc(band_width * centred)
    angles = 2.0 * math.pi * shift_bins.astype(jnp.float32)[..., None] * centred / bin_count
    taps = jnp.stack([lowpass * jnp.cos(angles), lowpass * jnp.sin(angles)], axis=-2)
    taps = taps.astype(jnp.bfloat16).astype(jnp.float32)
    zeros = jnp.zeros(taps.shape[:-1] + (64,), jnp.float32)
    return jnp.concatenate([taps[..., 32:], zeros, taps[..., :32]], axis=-1)


def circulant(row):
    block = jnp.broadcast_to(row, (32, lanes))
    parts = [pltpu.roll(block, phase, 1, stride=4, stride_axis=0) for phase in range(4)]
    return jnp.concatenate(parts, axis=0).T


def build_weights(taps_ref, weight_ref):
    real_part = circulant(taps_ref[0, 0:1, :])
    imag_part = circulant(taps_ref[0, 1:2, :])
    k = lax.broadcasted_iota(jnp.int32, (lanes, lanes), 0)
    c = lax.broadcasted_iota(jnp.int32, (lanes, lanes), 1)
    t = 4 * (c & 31) + (c >> 5)
    inside = jnp.abs(k - t) < 64
    for place, mask in ((0, inside), (1, jnp.logical_not(inside))):
        re = jnp.where(mask, real_part, 0.0)
        im = jnp.where(mask, imag_part, 0.0)
        weight_ref[place, 0:lanes, 0:lanes] = re.astype(jnp.bfloat16)
        weight_ref[place, 0:lanes, lanes:] = im.astype(jnp.bfloat16)
        weight_ref[place, lanes:, 0:lanes] = (-im).astype(jnp.bfloat16)
        weight_ref[place, lanes:, lanes:] = re.astype(jnp.bfloat16)


def looks_kernel(
    row_step, slots_ref, taps_ref, first_ref, second_ref, looks_ref, low_ref, high_ref, weight_ref, band_ref
):
    rows, tiles = first_ref.shape[1], first_ref.shape[2]
    build_weights(taps_ref, weight_ref)
    lane = lax.broadcasted_iota(jnp.int32, (segments, 2 * lanes), 1) & (lanes - 1)
    segment = lax.broadcasted_iota(jnp.int32, (segments, 2 * lanes), 0)
    from_before = jnp.where(lane >= 64, 1.0, 0.0).astype(jnp.bfloat16)
    from_after = jnp.where(lane < 64, 1.0, 0.0).astype(jnp.bfloat16)

    def filter_rows(source_ref, start, slot):
        current, edges = [], []
        for i in range(row_step):
            x = [source_ref[0, start + i, q] for q in range(tiles)]
            head = pltpu.roll(x[-1].astype(jnp.float32), 1, 0)
            head = jnp.where(segment == 0, 0.0, head).astype(jnp.bfloat16)
            tail = pltpu.roll(x[0].astype(jnp.float32), segments - 1, 0)
            tail = jnp.where(segment == segments - 1, 0.0, tail).astype(jnp.bfloat16)
            y = [head] + x + [tail]
            current += x
            edges += [y[q] * from_before + y[q + 2] * from_after for q in range(tiles)]
        current = jnp.concatenate(current, axis=0)
        edges = jnp.concatenate(edges, axis=0)
        out = jnp.dot(current, weight_ref[0], preferred_element_type=jnp.float32)
        out = out + jnp.dot(edges, weight_ref[1], preferred_element_type=jnp.float32)
        band_ref[slot] = out.astype(jnp.bfloat16).reshape(row_step, tiles, segments, 2 * lanes)

    group = lax.broadcasted_iota(jnp.int32, (segments, lanes), 1) >> 5
    outer = (group == 0) | (group == 3)
    lower = group < 2
    even = (group & 1) == 0

    def pool(v):
        a = jnp.where(outer, v[0], v[2]) + pltpu.roll(jnp.where(outer, v[2], v[0]), 64, 1)
        b = jnp.where(lower, v[1], v[3]) + pltpu.roll(jnp.where(lower, v[3], v[1]), 64, 1)
        return jnp.where(even, a, b) + pltpu.roll(jnp.where(even, b, a), 32, 1)

    def step(index, carry):
        start = index * row_step
        filter_rows(first_ref, start, 0)
        filter_rows(second_ref, start, 1)
        for i in range(row_step):
            for a in range(tiles // 4):
                planes = [[], [], [], []]
                for b in range(4):
                    q = 4 * a + b
                    one = band_ref[0, i, q].astype(jnp.float32)
                    two = band_ref[1, i, q].astype(jnp.float32)
                    fr, fi = one[:, :lanes], one[:, lanes:]
                    sr, si = two[:, :lanes], two[:, lanes:]
                    planes[0].append(fr * sr + fi * si)
                    planes[1].append(fi * sr - fr * si)
                    planes[2].append(fr * fr + fi * fi)
                    planes[3].append(sr * sr + si * si)
                for p in range(4):
                    looks_ref[0, start + i, p, a] = pool(planes[p])
        return carry

    lax.fori_loop(0, rows // row_step, step, 0)
    low_ref[...] = looks_ref[:, rows - below :].astype(jnp.bfloat16)
    high_ref[...] = looks_ref[:, :above].astype(jnp.bfloat16)


def pair_looks(slots, taps, own, other):
    dates, rows, tiles = own.shape[:3]
    row_step = 4
    tail = (4, tiles // 4, segments, lanes)
    image = (1, rows, tiles, segments, 2 * lanes)
    return pl.pallas_call(
        lambda *refs: looks_kernel(row_step, *refs),
        out_shape=(
            jax.ShapeDtypeStruct((dates, rows) + tail, jnp.float32),
            jax.ShapeDtypeStruct((dates, below) + tail, jnp.bfloat16),
            jax.ShapeDtypeStruct((dates, above) + tail, jnp.bfloat16),
        ),
        grid_spec=pltpu.PrefetchScalarGridSpec(
            num_scalar_prefetch=1,
            grid=(dates,),
            in_specs=[
                pl.BlockSpec((1, 2, lanes), lambda i, s: (i, 0, 0)),
                pl.BlockSpec(image, lambda i, s: (i, 0, 0, 0, 0)),
                pl.BlockSpec(image, lambda i, s: (s[i], 0, 0, 0, 0)),
            ],
            out_specs=[
                pl.BlockSpec((1, n) + tail, lambda i, s: (i, 0, 0, 0, 0, 0)) for n in (rows, below, above)
            ],
            scratch_shapes=[
                pltpu.VMEM((2, 2 * lanes, 2 * lanes), jnp.bfloat16),
                pltpu.VMEM((2, row_step, tiles, segments, 2 * lanes), jnp.bfloat16),
            ],
        ),
        compiler_params=pltpu.CompilerParams(vmem_limit_bytes=40 << 20),
        cost_estimate=pl.CostEstimate(
            flops=dates * rows * tiles * segments * 2 * 2 * 512 * 256,
            bytes_accessed=dates * rows * tiles * segments * 256 * 8,
            transcendentals=0,
        ),
        name="looks",
    )(slots, taps, own, other)


def finish_kernel(looks_ref, low_ref, high_ref, *rest):
    cross_ref, coherence_ref, turn_ref = rest[-3:]
    rows, halves = looks_ref.shape[1], looks_ref.shape[3]
    for a in range(halves):
        for h in range(0, segments, 8):
            window = []
            for p in range(4):
                e = [low_ref[0, i, p, a].astype(jnp.float32)[h : h + 8] for i in range(below)]
                e += [looks_ref[0, i, p, a, h : h + 8, :] for i in range(rows)]
                e += [high_ref[0, i, p, a].astype(jnp.float32)[h : h + 8] for i in range(above)]
                s2 = [e[i] + e[i + 1] for i in range(len(e) - 1)]
                s4 = [s2[i] + s2[i + 2] for i in range(len(s2) - 2)]
                s8 = [s4[i] + s4[i + 4] for i in range(len(s4) - 4)]
                window.append([s8[r] + s8[r + 8] + s4[r + 16] for r in range(rows)])
            for r in range(rows):
                cr, ci, pf, ps = (window[p][r] for p in range(4))
                spot = pl.ds(h * rows + r, 8, stride=rows)
                turn_ref[0, spot, :] = cr / 80.0
                turn_ref[1, spot, :] = ci / 80.0
                turn_ref[2, spot, :] = jnp.sqrt(cr * cr + ci * ci) * lax.rsqrt(pf * ps + epsilon)
        for s in range(segments):
            column = (s * halves + a) * lanes
            for k in range(2):
                cross_ref[0, 0, k, :, column : column + lanes] = turn_ref[
                    k, s * rows : (s + 1) * rows, :
                ].astype(jnp.bfloat16)
            coherence_ref[0, 0, :, column : column + lanes] = turn_ref[
                2, s * rows : (s + 1) * rows, :
            ].astype(jnp.bfloat16)


def finish(match, looks, low, high, so_far):
    dates, rows = looks.shape[:2]
    tail = looks.shape[2:]
    columns = tail[1] * segments * lanes
    block = lambda n: pl.BlockSpec((1, n) + tail, lambda i: (i, 0, 0, 0, 0, 0))
    anywhere = pl.BlockSpec(memory_space=pl.ANY)
    return pl.pallas_call(
        finish_kernel,
        out_shape=(
            jax.ShapeDtypeStruct((2, dates, 2, rows, columns), jnp.bfloat16),
            jax.ShapeDtypeStruct((2, dates, rows, columns), jnp.bfloat16),
        ),
        grid=(dates,),
        in_specs=[block(rows), block(below), block(above)] + [anywhere] * len(so_far),
        out_specs=[
            pl.BlockSpec((1, 1, 2, rows, columns), lambda i: (match, i, 0, 0, 0)),
            pl.BlockSpec((1, 1, rows, columns), lambda i: (match, i, 0, 0)),
        ],
        scratch_shapes=[pltpu.VMEM((3, segments * rows, lanes), jnp.float32)],
        input_output_aliases={3 + i: i for i in range(len(so_far))},
        compiler_params=pltpu.CompilerParams(vmem_limit_bytes=40 << 20),
        cost_estimate=pl.CostEstimate(
            flops=dates * rows * columns * 40, bytes_accessed=dates * rows * columns * 32, transcendentals=0
        ),
        name="finish",
    )(looks, low, high, *so_far)


def per_device(acquisitions, partners, band_shifts):
    dates, rows, _, samples = acquisitions.shape
    tiles = samples // (segments * lanes)
    top_bit = lax.axis_size("date").bit_length() - 2
    strips = lax.axis_size("strip")
    upward = [(i, i + 1) for i in range(strips - 1)]
    downward = [(i + 1, i) for i in range(strips - 1)]
    taps = make_taps(band_shifts)
    slots = partners % dates
    own = acquisitions.reshape(dates, rows, 2, segments, tiles, lanes)
    own = own.transpose(0, 1, 4, 3, 2, 5).reshape(dates, rows, tiles, segments, 2 * lanes)
    far = partner(own, "date", top_bit)
    near = partner(own, "date", 0)
    results = ()
    for match, other in ((0, near), (1, far)):
        looks, low, high = pair_looks(slots[match], taps[match], own, other)
        low = lax.ppermute(low, "strip", upward)
        high = lax.ppermute(high, "strip", downward)
        results = finish(match, looks, low, high, results)
    return tuple(results)


def solution(mesh):
    in_specs = (
        P(("grp", "date"), "strip", None, None),
        P(None, ("grp", "date")),
        P(None, ("grp", "date")),
    )
    out_specs = (
        P(None, ("grp", "date"), None, "strip", None),
        P(None, ("grp", "date"), "strip", None),
    )
    return jax.shard_map(
        per_device, mesh=mesh, in_specs=in_specs, out_specs=out_specs, check_vma=False
    )
```

```python
import math

import jax
import jax.numpy as jnp
from jax import lax
from jax.experimental import pallas as pl
from jax.experimental.layout import Layout, with_layout_constraint

from jax.experimental.pallas import tpu as pltpu
from jax.sharding import PartitionSpec as P

band_width = 0.8
bin_count = 256.0
epsilon = 1e-06
below = 10
above = 9
lanes = 128
segments = 16


def partner(block, axis, distance):
    count = lax.axis_size(axis)
    route = []
    for low in range(count):
        high = low | 1 << distance
        if high != low and high < count:
            route += [(low, high), (high, low)]
    return lax.ppermute(block, axis, route)


def make_taps(shift_bins):
    positions = jnp.arange(64, dtype=jnp.float32)
    centred = positions - 31.5
    hamming = 0.54 - 0.46 * jnp.cos(2.0 * math.pi * positions / 63.0)
    lowpass = hamming * band_width * jnp.sinc(band_width * centred)
    angles = 2.0 * math.pi * shift_bins.astype(jnp.float32)[..., None] * centred / bin_count
    taps = jnp.stack([lowpass * jnp.cos(angles), lowpass * jnp.sin(angles)], axis=-2)
    taps = taps.astype(jnp.bfloat16).astype(jnp.float32)
    zeros = jnp.zeros(taps.shape[:-1] + (64,), jnp.float32)
    return jnp.concatenate([taps[..., 32:], zeros, taps[..., :32]], axis=-1)


def circulant(row):
    block = jnp.broadcast_to(row, (32, lanes))
    parts = [pltpu.roll(block, phase, 1, stride=4, stride_axis=0) for phase in range(4)]
    return jnp.concatenate(parts, axis=0).T


def build_weights(taps_ref, weight_ref):
    real_part = circulant(taps_ref[0, 0:1, :])
    imag_part = circulant(taps_ref[0, 1:2, :])
    k = lax.broadcasted_iota(jnp.int32, (lanes, lanes), 0)
    c = lax.broadcasted_iota(jnp.int32, (lanes, lanes), 1)
    t = 4 * (c & 31) + (c >> 5)
    inside = jnp.abs(k - t) < 64
    for place, mask in ((0, inside), (1, jnp.logical_not(inside))):
        re = jnp.where(mask, real_part, 0.0)
        im = jnp.where(mask, imag_part, 0.0)
        weight_ref[place, 0:lanes, 0:lanes] = re.astype(jnp.bfloat16)
        weight_ref[place, 0:lanes, lanes:] = im.astype(jnp.bfloat16)
        weight_ref[place, lanes:, 0:lanes] = (-im).astype(jnp.bfloat16)
        weight_ref[place, lanes:, lanes:] = re.astype(jnp.bfloat16)


def looks_kernel(
    row_step, firsts_ref, seconds_ref, taps_ref, first_ref, second_ref, looks_ref, low_ref, high_ref, weight_ref, band_ref
):
    rows, tiles = first_ref.shape[1], first_ref.shape[2]
    build_weights(taps_ref, weight_ref)
    lane = lax.broadcasted_iota(jnp.int32, (segments, 2 * lanes), 1) & (lanes - 1)
    segment = lax.broadcasted_iota(jnp.int32, (segments, 2 * lanes), 0)
    from_before = jnp.where(lane >= 64, 1.0, 0.0).astype(jnp.bfloat16)
    from_after = jnp.where(lane < 64, 1.0, 0.0).astype(jnp.bfloat16)

    def filter_rows(source_ref, start, slot):
        current, edges = [], []
        for i in range(row_step):
            x = [source_ref[0, start + i, q] for q in range(tiles)]
            head = pltpu.roll(x[-1].astype(jnp.float32), 1, 0)
            head = jnp.where(segment == 0, 0.0, head).astype(jnp.bfloat16)
            tail = pltpu.roll(x[0].astype(jnp.float32), segments - 1, 0)
            tail = jnp.where(segment == segments - 1, 0.0, tail).astype(jnp.bfloat16)
            y = [head] + x + [tail]
            current += x
            edges += [y[q] * from_before + y[q + 2] * from_after for q in range(tiles)]
        current = jnp.concatenate(current, axis=0)
        edges = jnp.concatenate(edges, axis=0)
        out = jnp.dot(current, weight_ref[0], preferred_element_type=jnp.float32)
        out = out + jnp.dot(edges, weight_ref[1], preferred_element_type=jnp.float32)
        band_ref[slot] = out.astype(jnp.bfloat16).reshape(row_step, tiles, segments, 2 * lanes)

    group = lax.broadcasted_iota(jnp.int32, (segments, lanes), 1) >> 5
    outer = (group == 0) | (group == 3)
    lower = group < 2
    even = (group & 1) == 0

    def pool(v):
        a = jnp.where(outer, v[0], v[2]) + pltpu.roll(jnp.where(outer, v[2], v[0]), 64, 1)
        b = jnp.where(lower, v[1], v[3]) + pltpu.roll(jnp.where(lower, v[3], v[1]), 64, 1)
        return jnp.where(even, a, b) + pltpu.roll(jnp.where(even, b, a), 32, 1)

    def step(index, carry):
        start = index * row_step
        filter_rows(first_ref, start, 0)
        filter_rows(second_ref, start, 1)
        for i in range(row_step):
            for a in range(tiles // 4):
                planes = [[], [], [], []]
                for b in range(4):
                    q = 4 * a + b
                    one = band_ref[0, i, q].astype(jnp.float32)
                    two = band_ref[1, i, q].astype(jnp.float32)
                    fr, fi = one[:, :lanes], one[:, lanes:]
                    sr, si = two[:, :lanes], two[:, lanes:]
                    planes[0].append(fr * sr + fi * si)
                    planes[1].append(fi * sr - fr * si)
                    planes[2].append(fr * fr + fi * fi)
                    planes[3].append(sr * sr + si * si)
                for p in range(4):
                    looks_ref[0, start + i, p, a] = pool(planes[p])
        return carry

    lax.fori_loop(0, rows // row_step, step, 0)
    low_ref[...] = looks_ref[:, rows - below :].astype(jnp.bfloat16)
    high_ref[...] = looks_ref[:, :above].astype(jnp.bfloat16)


def pair_looks(firsts, seconds, taps, own, other):
    dates = firsts.shape[0]
    rows, tiles = own.shape[1:3]
    row_step = 4
    tail = (4, tiles // 4, segments, lanes)
    image = (1, rows, tiles, segments, 2 * lanes)
    return pl.pallas_call(
        lambda *refs: looks_kernel(row_step, *refs),
        out_shape=(
            jax.ShapeDtypeStruct((dates, rows) + tail, jnp.float32),
            jax.ShapeDtypeStruct((dates, below) + tail, jnp.bfloat16),
            jax.ShapeDtypeStruct((dates, above) + tail, jnp.bfloat16),
        ),
        grid_spec=pltpu.PrefetchScalarGridSpec(
            num_scalar_prefetch=2,
            grid=(dates,),
            in_specs=[
                pl.BlockSpec((1, 2, lanes), lambda i, f, s: (f[i], 0, 0)),
                pl.BlockSpec(image, lambda i, f, s: (f[i], 0, 0, 0, 0)),
                pl.BlockSpec(image, lambda i, f, s: (s[i], 0, 0, 0, 0)),
            ],
            out_specs=[
                pl.BlockSpec((1, n) + tail, lambda i, f, s: (i, 0, 0, 0, 0, 0)) for n in (rows, below, above)
            ],
            scratch_shapes=[
                pltpu.VMEM((2, 2 * lanes, 2 * lanes), jnp.bfloat16),
                pltpu.VMEM((2, row_step, tiles, segments, 2 * lanes), jnp.bfloat16),
            ],
        ),
        compiler_params=pltpu.CompilerParams(vmem_limit_bytes=14 << 20),
        cost_estimate=pl.CostEstimate(
            flops=dates * rows * tiles * segments * 2 * 2 * 512 * 256,
            bytes_accessed=dates * rows * tiles * segments * 256 * 8,
            transcendentals=0,
        ),
        name="looks",
    )(firsts, seconds, taps, own, other)


def finish_kernel(places_ref, looks_ref, low_ref, high_ref, *rest):
    cross_ref, coherence_ref, turn_ref = rest[-3:]
    rows, halves = looks_ref.shape[1], looks_ref.shape[3]
    for a in range(halves):
        for h in range(0, segments, 8):
            window = []
            for p in range(4):
                e = [low_ref[0, i, p, a].astype(jnp.float32)[h : h + 8] for i in range(below)]
                e += [looks_ref[0, i, p, a, h : h + 8, :] for i in range(rows)]
                e += [high_ref[0, i, p, a].astype(jnp.float32)[h : h + 8] for i in range(above)]
                s2 = [e[i] + e[i + 1] for i in range(len(e) - 1)]
                s4 = [s2[i] + s2[i + 2] for i in range(len(s2) - 2)]
                s8 = [s4[i] + s4[i + 4] for i in range(len(s4) - 4)]
                window.append([s8[r] + s8[r + 8] + s4[r + 16] for r in range(rows)])
            for r in range(rows):
                cr, ci, pf, ps = (window[p][r] for p in range(4))
                spot = pl.ds(h * rows + r, 8, stride=rows)
                turn_ref[0, spot, :] = cr / 80.0
                turn_ref[1, spot, :] = ci / 80.0
                turn_ref[2, spot, :] = jnp.sqrt(cr * cr + ci * ci) * lax.rsqrt(pf * ps + epsilon)
        for s in range(segments):
            column = (s * halves + a) * lanes
            for k in range(2):
                cross_ref[0, 0, k, :, column : column + lanes] = turn_ref[
                    k, s * rows : (s + 1) * rows, :
                ].astype(jnp.bfloat16)
            coherence_ref[0, 0, :, column : column + lanes] = turn_ref[
                2, s * rows : (s + 1) * rows, :
            ].astype(jnp.bfloat16)


def finish(match, places, dates, looks, low, high, so_far):
    count, rows = looks.shape[:2]
    tail = looks.shape[2:]
    columns = tail[1] * segments * lanes
    block = lambda n: pl.BlockSpec((1, n) + tail, lambda i, p: (i, 0, 0, 0, 0, 0))
    anywhere = pl.BlockSpec(memory_space=pl.ANY)
    return pl.pallas_call(
        finish_kernel,
        out_shape=(
            jax.ShapeDtypeStruct((2, dates, 2, rows, columns), jnp.bfloat16),
            jax.ShapeDtypeStruct((2, dates, rows, columns), jnp.bfloat16),
        ),
        grid_spec=pltpu.PrefetchScalarGridSpec(
            num_scalar_prefetch=1,
            grid=(count,),
            in_specs=[block(rows), block(below), block(above)] + [anywhere] * len(so_far),
            out_specs=[
                pl.BlockSpec((1, 1, 2, rows, columns), lambda i, p: (match, p[i], 0, 0, 0)),
                pl.BlockSpec((1, 1, rows, columns), lambda i, p: (match, p[i], 0, 0)),
            ],
            scratch_shapes=[pltpu.VMEM((3, segments * rows, lanes), jnp.float32)],
        ),
        input_output_aliases={4 + i: i for i in range(len(so_far))},
        compiler_params=pltpu.CompilerParams(vmem_limit_bytes=10 << 20),
        cost_estimate=pl.CostEstimate(
            flops=count * rows * columns * 40, bytes_accessed=count * rows * columns * 32, transcendentals=0
        ),
        name="finish",
    )(places, looks, low, high, *so_far)


def arrange(images):
    dates, rows, _, samples = images.shape
    tiles = samples // (segments * lanes)
    images = images.reshape(dates, rows, 2, segments, tiles, lanes)
    images = with_layout_constraint(images, Layout(major_to_minor=(0, 1, 3, 4, 2, 5)))
    return images.transpose(0, 1, 4, 3, 2, 5).reshape(dates, rows, tiles, segments, 2 * lanes)


def per_device(acquisitions, partners, band_shifts):
    dates = acquisitions.shape[0]
    top_bit = lax.axis_size("date").bit_length() - 2
    strips = lax.axis_size("strip")
    upward = [(i, i + 1) for i in range(strips - 1)]
    downward = [(i + 1, i) for i in range(strips - 1)]
    far = [partner(acquisitions[k : k + 1], "date", top_bit) for k in range(dates)]
    taps = make_taps(band_shifts)
    slots = partners % dates
    every = jnp.arange(dates, dtype=jnp.int32)
    own_of_slot = jnp.sum(jnp.where(slots[1][None, :] == every[:, None], every[None, :], 0), axis=1)
    own = arrange(acquisitions)
    near = partner(own, "date", 0)

    def halos(parts):
        looks, low, high = parts
        return looks, lax.ppermute(low, "strip", upward), lax.ppermute(high, "strip", downward)

    pending = [(0, every) + halos(pair_looks(every, slots[0], taps[0], own, near))]
    for k in range(dates):
        place = own_of_slot[k : k + 1]
        pair = pair_looks(place, jnp.zeros((1,), jnp.int32), taps[1], own, arrange(far[k]))
        pending.append((1, place) + halos(pair))
    results = ()
    for match, place, looks, low, high in pending:
        results = finish(match, place, dates, looks, low, high, results)
    return tuple(results)


def solution(mesh):
    in_specs = (
        P(("grp", "date"), "strip", None, None),
        P(None, ("grp", "date")),
        P(None, ("grp", "date")),
    )
    out_specs = (
        P(None, ("grp", "date"), None, "strip", None),
        P(None, ("grp", "date"), "strip", None),
    )
    return jax.shard_map(
        per_device, mesh=mesh, in_specs=in_specs, out_specs=out_specs, check_vma=False
    )
```

```python
import math

import jax
import jax.numpy as jnp
from jax import lax
from jax.experimental import pallas as pl
from jax.experimental.layout import Layout, with_layout_constraint

from jax.experimental.pallas import tpu as pltpu
from jax.sharding import PartitionSpec as P

band_width = 0.8
bin_count = 256.0
epsilon = 1e-06
below = 10
above = 9
row_step = 2
in_flight = 3
lanes = 128
segments = 16


def make_taps(shift_bins):
    positions = jnp.arange(64, dtype=jnp.float32)
    centred = positions - 31.5
    hamming = 0.54 - 0.46 * jnp.cos(2.0 * math.pi * positions / 63.0)
    lowpass = hamming * band_width * jnp.sinc(band_width * centred)
    angles = 2.0 * math.pi * shift_bins.astype(jnp.float32)[..., None] * centred / bin_count
    taps = jnp.stack([lowpass * jnp.cos(angles), lowpass * jnp.sin(angles)], axis=-2)
    taps = taps.astype(jnp.bfloat16).astype(jnp.float32)
    zeros = jnp.zeros(taps.shape[:-1] + (64,), jnp.float32)
    return jnp.concatenate([taps[..., 32:], zeros, taps[..., :32]], axis=-1)


def circulant(row):
    block = jnp.broadcast_to(row, (32, lanes))
    parts = [pltpu.roll(block, phase, 1, stride=4, stride_axis=0) for phase in range(4)]
    return jnp.concatenate(parts, axis=0).T


def build_weights(taps_ref, weight_ref, spot):
    real_part = circulant(taps_ref[spot, 0:1, :])
    imag_part = circulant(taps_ref[spot, 1:2, :])
    k = lax.broadcasted_iota(jnp.int32, (lanes, lanes), 0)
    c = lax.broadcasted_iota(jnp.int32, (lanes, lanes), 1)
    t = 4 * (c & 31) + (c >> 5)
    inside = jnp.abs(k - t) < 64
    for place, mask in ((0, inside), (1, jnp.logical_not(inside))):
        re = jnp.where(mask, real_part, 0.0)
        im = jnp.where(mask, imag_part, 0.0)
        weight_ref[spot, place, 0:lanes, 0:lanes] = re.astype(jnp.bfloat16)
        weight_ref[spot, place, 0:lanes, lanes:] = im.astype(jnp.bfloat16)
        weight_ref[spot, place, lanes:, 0:lanes] = (-im).astype(jnp.bfloat16)
        weight_ref[spot, place, lanes:, lanes:] = re.astype(jnp.bfloat16)


def exchange_kernel(
    groups, strips, own_of_slot_ref, taps_ref, own_ref, looks_ref, low_ref, high_ref,
    got_ref, weight_ref, band_ref, low_out_ref, high_out_ref,
    got_send, got_recv, low_send, low_recv, high_send, high_recv,
):
    slots, rows, tiles = own_ref.shape[:3]
    chunks = rows // row_step
    low_first = (rows - below) // row_step
    high_last = (above - 1) // row_step
    me = lax.axis_index("date")
    strip = lax.axis_index("strip")
    peers = (me + 1 - 2 * lax.rem(me, 2), lax.rem(me + groups // 2, groups))
    can_up = strip < strips - 1
    can_down = strip > 0

    barrier = pltpu.get_barrier_semaphore()
    for peer in peers:
        pl.semaphore_signal(barrier, inc=1, device_id={"date": peer}, device_id_type=pl.DeviceIdType.MESH)

    @pl.when(can_up)
    def _():
        pl.semaphore_signal(barrier, inc=1, device_id={"strip": strip + 1}, device_id_type=pl.DeviceIdType.MESH)

    @pl.when(can_down)
    def _():
        pl.semaphore_signal(barrier, inc=1, device_id={"strip": strip - 1}, device_id_type=pl.DeviceIdType.MESH)

    pl.semaphore_wait(barrier, 2 + can_up.astype(jnp.int32) + can_down.astype(jnp.int32))

    def chunk_of(step):
        half = step // (chunks // 2)
        return (chunks - 1 - step) * (1 - half) + (step - chunks // 2) * half

    def date_copy(match, chunk):
        spot = pl.ds(chunk * row_step, row_step)
        return pltpu.make_async_remote_copy(
            src_ref=own_ref.at[:, spot],
            dst_ref=got_ref.at[match, :, spot],
            send_sem=got_send.at[match, chunk],
            recv_sem=got_recv.at[match, chunk],
            device_id={"date": peers[match]},
            device_id_type=pl.DeviceIdType.MESH,
        )

    def low_copy(match, chunk):
        spot = pl.ds((chunk - low_first) * row_step, row_step)
        return pltpu.make_async_remote_copy(
            src_ref=low_out_ref.at[match, spot],
            dst_ref=low_ref.at[match, spot],
            send_sem=low_send.at[match, chunk],
            recv_sem=low_recv.at[match, chunk],
            device_id={"strip": strip + 1},
            device_id_type=pl.DeviceIdType.MESH,
        )

    def high_copy(match, chunk):
        spot = pl.ds(chunk * row_step, row_step)
        return pltpu.make_async_remote_copy(
            src_ref=high_out_ref.at[match, spot],
            dst_ref=high_ref.at[match, spot],
            send_sem=high_send.at[match, chunk],
            recv_sem=high_recv.at[match, chunk],
            device_id={"strip": strip - 1},
            device_id_type=pl.DeviceIdType.MESH,
        )

    def start_dates(match):
        def body(step, carry):
            date_copy(match, chunk_of(step)).start()
            return carry

        return body

    lax.fori_loop(0, chunks, start_dates(0), 0)
    lax.fori_loop(0, in_flight, start_dates(1), 0)

    @pl.when(strip == 0)
    def _():
        low_ref[...] = jnp.zeros(low_ref.shape, low_ref.dtype)

    @pl.when(strip == strips - 1)
    def _():
        high_ref[...] = jnp.zeros(high_ref.shape, high_ref.dtype)

    def weigh(spot, carry):
        build_weights(taps_ref, weight_ref, spot)
        return carry

    lax.fori_loop(0, 2 * slots, weigh, 0)

    lane = lax.broadcasted_iota(jnp.int32, (segments, 2 * lanes), 1) & (lanes - 1)
    segment = lax.broadcasted_iota(jnp.int32, (segments, 2 * lanes), 0)
    from_before = jnp.where(lane >= 64, 1.0, 0.0).astype(jnp.bfloat16)
    from_after = jnp.where(lane < 64, 1.0, 0.0).astype(jnp.bfloat16)

    def filter_rows(load, spot, band):
        current, edges = [], []
        for i in range(row_step):
            x = [load(i, q) for q in range(tiles)]
            head = pltpu.roll(x[-1].astype(jnp.float32), 1, 0)
            head = jnp.where(segment == 0, 0.0, head).astype(jnp.bfloat16)
            tail = pltpu.roll(x[0].astype(jnp.float32), segments - 1, 0)
            tail = jnp.where(segment == segments - 1, 0.0, tail).astype(jnp.bfloat16)
            y = [head] + x + [tail]
            current += x
            edges += [y[q] * from_before + y[q + 2] * from_after for q in range(tiles)]
        current = jnp.concatenate(current, axis=0)
        edges = jnp.concatenate(edges, axis=0)
        out = jnp.dot(current, weight_ref[spot, 0], preferred_element_type=jnp.float32)
        out = out + jnp.dot(edges, weight_ref[spot, 1], preferred_element_type=jnp.float32)
        band_ref[band] = out.astype(jnp.bfloat16).reshape(row_step, tiles, segments, 2 * lanes)

    group = lax.broadcasted_iota(jnp.int32, (segments, lanes), 1) >> 5
    outer = (group == 0) | (group == 3)
    lower = group < 2
    even = (group & 1) == 0

    def pool(v):
        a = jnp.where(outer, v[0], v[2]) + pltpu.roll(jnp.where(outer, v[2], v[0]), 64, 1)
        b = jnp.where(lower, v[1], v[3]) + pltpu.roll(jnp.where(lower, v[3], v[1]), 64, 1)
        return jnp.where(even, a, b) + pltpu.roll(jnp.where(even, b, a), 32, 1)

    def run(match):
        def body(step, carry):
            chunk = chunk_of(step)
            start = chunk * row_step
            date_copy(match, chunk).wait_recv()
            if match == 1:
                date_copy(match, chunk).wait_send()

                @pl.when(step + in_flight < chunks)
                def _():
                    date_copy(match, chunk_of(step + in_flight)).start()

            for slot in range(slots):
                place = own_of_slot_ref[match, slot]
                spot = match * slots + slot
                filter_rows(lambda i, q: own_ref[place, start + i, q], spot, 2 * slot)
                filter_rows(lambda i, q: got_ref[match, slot, start + i, q], spot, 2 * slot + 1)
            for slot in range(slots):
                for i in range(row_step):
                    for a in range(tiles // 4):
                        planes = [[], [], [], []]
                        for b in range(4):
                            q = 4 * a + b
                            one = band_ref[2 * slot, i, q].astype(jnp.float32)
                            two = band_ref[2 * slot + 1, i, q].astype(jnp.float32)
                            fr, fi = one[:, :lanes], one[:, lanes:]
                            sr, si = two[:, :lanes], two[:, lanes:]
                            planes[0].append(fr * sr + fi * si)
                            planes[1].append(fi * sr - fr * si)
                            planes[2].append(fr * fr + fi * fi)
                            planes[3].append(sr * sr + si * si)
                        for p in range(4):
                            looks_ref[match, start + i, slot, p, a] = pool(planes[p])

            @pl.when((chunk >= low_first) & can_up)
            def _():
                low_out_ref[match, pl.ds((chunk - low_first) * row_step, row_step)] = looks_ref[
                    match, pl.ds(start, row_step)
                ].astype(jnp.bfloat16)
                low_copy(match, chunk).start()

            @pl.when((chunk <= high_last) & can_down)
            def _():
                high_out_ref[match, pl.ds(start, row_step)] = looks_ref[match, pl.ds(start, row_step)].astype(
                    jnp.bfloat16
                )
                high_copy(match, chunk).start()

            return carry

        return body

    for match in range(2):
        lax.fori_loop(0, chunks, run(match), 0)

    for match in range(2):

        def settle_low(chunk, carry):
            @pl.when(can_up)
            def _():
                low_copy(match, chunk).wait_send()

            @pl.when(can_down)
            def _():
                low_copy(match, chunk).wait_recv()

            return carry

        def settle_high(chunk, carry):
            @pl.when(can_down)
            def _():
                high_copy(match, chunk).wait_send()

            @pl.when(can_up)
            def _():
                high_copy(match, chunk).wait_recv()

            return carry

        lax.fori_loop(low_first, chunks, settle_low, 0)
        lax.fori_loop(0, high_last + 1, settle_high, 0)

    def settle_near(chunk, carry):
        date_copy(0, chunk).wait_send()
        return carry

    lax.fori_loop(0, chunks, settle_near, 0)


def exchange(own_of_slot, taps, own):
    slots, rows, tiles = own.shape[:3]
    chunks = rows // row_step
    groups, strips = lax.axis_size("date"), lax.axis_size("strip")
    tail = (slots, 4, tiles // 4, segments, lanes)
    high_rows = ((above - 1) // row_step + 1) * row_step
    in_vmem = pl.BlockSpec(memory_space=pltpu.VMEM)
    semaphores = pltpu.SemaphoreType.DMA((2, chunks))
    return pl.pallas_call(
        lambda *refs: exchange_kernel(groups, strips, *refs),
        out_shape=(
            jax.ShapeDtypeStruct((2, rows) + tail, jnp.float32),
            jax.ShapeDtypeStruct((2, below) + tail, jnp.bfloat16),
            jax.ShapeDtypeStruct((2, high_rows) + tail, jnp.bfloat16),
        ),
        in_specs=[pl.BlockSpec(memory_space=pltpu.SMEM), in_vmem, in_vmem],
        out_specs=[in_vmem] * 3,
        scratch_shapes=[
            pltpu.VMEM((2,) + own.shape, jnp.bfloat16),
            pltpu.VMEM((2 * slots, 2, 2 * lanes, 2 * lanes), jnp.bfloat16),
            pltpu.VMEM((2 * slots, row_step, tiles, segments, 2 * lanes), jnp.bfloat16),
            pltpu.VMEM((2, below) + tail, jnp.bfloat16),
            pltpu.VMEM((2, high_rows) + tail, jnp.bfloat16),
        ]
        + [semaphores] * 6,
        compiler_params=pltpu.CompilerParams(
            vmem_limit_bytes=36 << 20, collective_id=0, has_side_effects=True
        ),
        name="exchange",
    )(own_of_slot, taps, own)


def finish_kernel(places_ref, looks_ref, low_ref, high_ref, cross_ref, coherence_ref, turn_ref):
    rows, halves = looks_ref.shape[1], looks_ref.shape[4]
    for a in range(halves):
        for h in range(0, segments, 8):
            window = []
            for p in range(4):
                e = [low_ref[0, i, 0, p, a].astype(jnp.float32)[h : h + 8] for i in range(below)]
                e += [looks_ref[0, i, 0, p, a, h : h + 8, :] for i in range(rows)]
                e += [high_ref[0, i, 0, p, a].astype(jnp.float32)[h : h + 8] for i in range(above)]
                s2 = [e[i] + e[i + 1] for i in range(len(e) - 1)]
                s4 = [s2[i] + s2[i + 2] for i in range(len(s2) - 2)]
                s8 = [s4[i] + s4[i + 4] for i in range(len(s4) - 4)]
                window.append([s8[r] + s8[r + 8] + s4[r + 16] for r in range(rows)])
            for r in range(rows):
                cr, ci, pf, ps = (window[p][r] for p in range(4))
                spot = pl.ds(h * rows + r, 8, stride=rows)
                turn_ref[0, spot, :] = cr / 80.0
                turn_ref[1, spot, :] = ci / 80.0
                turn_ref[2, spot, :] = jnp.sqrt(cr * cr + ci * ci) * lax.rsqrt(pf * ps + epsilon)
        for s in range(segments):
            column = (s * halves + a) * lanes
            for k in range(2):
                cross_ref[0, 0, k, :, column : column + lanes] = turn_ref[
                    k, s * rows : (s + 1) * rows, :
                ].astype(jnp.bfloat16)
            coherence_ref[0, 0, :, column : column + lanes] = turn_ref[
                2, s * rows : (s + 1) * rows, :
            ].astype(jnp.bfloat16)


def finish(places, looks, low, high):
    matches, rows, dates = looks.shape[:3]
    tail = looks.shape[3:]
    columns = tail[1] * segments * lanes
    block = lambda n: pl.BlockSpec((1, n, 1) + tail, lambda m, i, p: (m, 0, i, 0, 0, 0, 0))
    return pl.pallas_call(
        finish_kernel,
        out_shape=(
            jax.ShapeDtypeStruct((matches, dates, 2, rows, columns), jnp.bfloat16),
            jax.ShapeDtypeStruct((matches, dates, rows, columns), jnp.bfloat16),
        ),
        grid_spec=pltpu.PrefetchScalarGridSpec(
            num_scalar_prefetch=1,
            grid=(matches, dates),
            in_specs=[block(rows), block(low.shape[1]), block(high.shape[1])],
            out_specs=[
                pl.BlockSpec((1, 1, 2, rows, columns), lambda m, i, p: (m, p[m, i], 0, 0, 0)),
                pl.BlockSpec((1, 1, rows, columns), lambda m, i, p: (m, p[m, i], 0, 0)),
            ],
            scratch_shapes=[pltpu.VMEM((3, segments * rows, lanes), jnp.float32)],
        ),
        compiler_params=pltpu.CompilerParams(vmem_limit_bytes=10 << 20),
        name="finish",
    )(places, looks, low, high)


def arrange(images):
    dates, rows, _, samples = images.shape
    tiles = samples // (segments * lanes)
    images = images.reshape(dates, rows, 2, segments, tiles, lanes)
    images = with_layout_constraint(images, Layout(major_to_minor=(0, 1, 3, 4, 2, 5)))
    return images.transpose(0, 1, 4, 3, 2, 5).reshape(dates, rows, tiles, segments, 2 * lanes)


def per_device(acquisitions, partners, band_shifts):
    dates = acquisitions.shape[0]
    slots = partners % dates
    every = jnp.arange(dates, dtype=jnp.int32)
    met = slots[:, None, :] == every[None, :, None]
    own_of_slot = jnp.sum(jnp.where(met, every[None, None, :], 0), axis=2)
    shifts = jnp.sum(jnp.where(met, band_shifts[:, None, :], 0), axis=2)
    taps = make_taps(shifts).reshape(2 * dates, 2, lanes)
    looks, low, high = exchange(own_of_slot, taps, arrange(acquisitions))
    return finish(own_of_slot, looks, low, high)


def solution(mesh):
    in_specs = (
        P(("grp", "date"), "strip", None, None),
        P(None, ("grp", "date")),
        P(None, ("grp", "date")),
    )
    out_specs = (
        P(None, ("grp", "date"), None, "strip", None),
        P(None, ("grp", "date"), "strip", None),
    )
    return jax.shard_map(
        per_device, mesh=mesh, in_specs=in_specs, out_specs=out_specs, check_vma=False
    )
```

```python
import math

import jax
import jax.numpy as jnp
from jax import lax
from jax.experimental import pallas as pl
from jax.experimental.layout import Layout, with_layout_constraint

from jax.experimental.pallas import tpu as pltpu
from jax.sharding import PartitionSpec as P

band_width = 0.8
bin_count = 256.0
epsilon = 1e-06
below = 10
above = 9
row_step = 2
in_flight = 3
lanes = 128
segments = 16


def make_taps(shift_bins):
    positions = jnp.arange(64, dtype=jnp.float32)
    centred = positions - 31.5
    hamming = 0.54 - 0.46 * jnp.cos(2.0 * math.pi * positions / 63.0)
    lowpass = hamming * band_width * jnp.sinc(band_width * centred)
    angles = 2.0 * math.pi * shift_bins.astype(jnp.float32)[..., None] * centred / bin_count
    taps = jnp.stack([lowpass * jnp.cos(angles), lowpass * jnp.sin(angles)], axis=-2)
    taps = taps.astype(jnp.bfloat16).astype(jnp.float32)
    zeros = jnp.zeros(taps.shape[:-1] + (64,), jnp.float32)
    return jnp.concatenate([taps[..., 32:], zeros, taps[..., :32]], axis=-1)


def circulant(row):
    block = jnp.broadcast_to(row, (32, lanes))
    parts = [pltpu.roll(block, phase, 1, stride=4, stride_axis=0) for phase in range(4)]
    return jnp.concatenate(parts, axis=0).T


def place_of(partners_ref, match, slot, dates):
    place = 0
    for i in range(1, dates):
        place = place + jnp.where(lax.rem(partners_ref[match, i], dates) == slot, i, 0)
    return place


def build_weights(taps_ref, weight_ref, spot, source):
    real_part = circulant(taps_ref[source, 0:1, :])
    imag_part = circulant(taps_ref[source, 1:2, :])
    k = lax.broadcasted_iota(jnp.int32, (lanes, lanes), 0)
    c = lax.broadcasted_iota(jnp.int32, (lanes, lanes), 1)
    t = 4 * (c & 31) + (c >> 5)
    inside = jnp.abs(k - t) < 64
    for place, mask in ((0, inside), (1, jnp.logical_not(inside))):
        re = jnp.where(mask, real_part, 0.0)
        im = jnp.where(mask, imag_part, 0.0)
        weight_ref[spot, place, 0:lanes, 0:lanes] = re.astype(jnp.bfloat16)
        weight_ref[spot, place, 0:lanes, lanes:] = im.astype(jnp.bfloat16)
        weight_ref[spot, place, lanes:, 0:lanes] = (-im).astype(jnp.bfloat16)
        weight_ref[spot, place, lanes:, lanes:] = re.astype(jnp.bfloat16)


def exchange_kernel(
    groups, strips, partners_ref, taps_ref, own_ref, looks_ref, low_ref, high_ref,
    got_ref, weight_ref, band_ref, low_out_ref, high_out_ref,
    got_send, got_recv, low_send, low_recv, high_send, high_recv,
):
    slots, rows, tiles = own_ref.shape[:3]
    chunks = rows // row_step
    low_first = (rows - below) // row_step
    high_last = (above - 1) // row_step
    me = lax.axis_index("date")
    strip = lax.axis_index("strip")
    peers = (me + 1 - 2 * lax.rem(me, 2), lax.rem(me + groups // 2, groups))
    can_up = strip < strips - 1
    can_down = strip > 0

    barrier = pltpu.get_barrier_semaphore()
    for peer in peers:
        pl.semaphore_signal(barrier, inc=1, device_id={"date": peer}, device_id_type=pl.DeviceIdType.MESH)

    @pl.when(can_up)
    def _():
        pl.semaphore_signal(barrier, inc=1, device_id={"strip": strip + 1}, device_id_type=pl.DeviceIdType.MESH)

    @pl.when(can_down)
    def _():
        pl.semaphore_signal(barrier, inc=1, device_id={"strip": strip - 1}, device_id_type=pl.DeviceIdType.MESH)

    pl.semaphore_wait(barrier, 2 + can_up.astype(jnp.int32) + can_down.astype(jnp.int32))

    def chunk_of(step):
        half = step // (chunks // 2)
        return (chunks - 1 - step) * (1 - half) + (step - chunks // 2) * half

    def date_copy(match, chunk):
        spot = pl.ds(chunk * row_step, row_step)
        return pltpu.make_async_remote_copy(
            src_ref=own_ref.at[:, spot],
            dst_ref=got_ref.at[match, :, spot],
            send_sem=got_send.at[match, chunk],
            recv_sem=got_recv.at[match, chunk],
            device_id={"date": peers[match]},
            device_id_type=pl.DeviceIdType.MESH,
        )

    def low_copy(match, chunk):
        spot = pl.ds((chunk - low_first) * row_step, row_step)
        return pltpu.make_async_remote_copy(
            src_ref=low_out_ref.at[match, spot],
            dst_ref=low_ref.at[match, spot],
            send_sem=low_send.at[match, chunk],
            recv_sem=low_recv.at[match, chunk],
            device_id={"strip": strip + 1},
            device_id_type=pl.DeviceIdType.MESH,
        )

    def high_copy(match, chunk):
        spot = pl.ds(chunk * row_step, row_step)
        return pltpu.make_async_remote_copy(
            src_ref=high_out_ref.at[match, spot],
            dst_ref=high_ref.at[match, spot],
            send_sem=high_send.at[match, chunk],
            recv_sem=high_recv.at[match, chunk],
            device_id={"strip": strip - 1},
            device_id_type=pl.DeviceIdType.MESH,
        )

    def start_dates(match):
        def body(step, carry):
            date_copy(match, chunk_of(step)).start()
            return carry

        return body

    lax.fori_loop(0, in_flight, start_dates(1), 0)
    lax.fori_loop(0, chunks, start_dates(0), 0)

    @pl.when(strip == 0)
    def _():
        low_ref[...] = jnp.zeros(low_ref.shape, low_ref.dtype)

    @pl.when(strip == strips - 1)
    def _():
        high_ref[...] = jnp.zeros(high_ref.shape, high_ref.dtype)

    def weigh(spot, carry):
        match = spot // slots
        place = place_of(partners_ref, match, lax.rem(spot, slots), slots)
        build_weights(taps_ref, weight_ref, spot, match * slots + place)
        return carry

    lax.fori_loop(0, 2 * slots, weigh, 0)

    lane = lax.broadcasted_iota(jnp.int32, (segments, 2 * lanes), 1) & (lanes - 1)
    segment = lax.broadcasted_iota(jnp.int32, (segments, 2 * lanes), 0)
    from_before = jnp.where(lane >= 64, 1.0, 0.0).astype(jnp.bfloat16)
    from_after = jnp.where(lane < 64, 1.0, 0.0).astype(jnp.bfloat16)

    def filter_rows(load, spot, band):
        current, edges = [], []
        for i in range(row_step):
            x = [load(i, q) for q in range(tiles)]
            head = pltpu.roll(x[-1].astype(jnp.float32), 1, 0)
            head = jnp.where(segment == 0, 0.0, head).astype(jnp.bfloat16)
            tail = pltpu.roll(x[0].astype(jnp.float32), segments - 1, 0)
            tail = jnp.where(segment == segments - 1, 0.0, tail).astype(jnp.bfloat16)
            y = [head] + x + [tail]
            current += x
            edges += [y[q] * from_before + y[q + 2] * from_after for q in range(tiles)]
        current = jnp.concatenate(current, axis=0)
        edges = jnp.concatenate(edges, axis=0)
        out = jnp.dot(current, weight_ref[spot, 0], preferred_element_type=jnp.float32)
        out = out + jnp.dot(edges, weight_ref[spot, 1], preferred_element_type=jnp.float32)
        band_ref[band] = out.astype(jnp.bfloat16).reshape(row_step, tiles, segments, 2 * lanes)

    group = lax.broadcasted_iota(jnp.int32, (segments, lanes), 1) >> 5
    outer = (group == 0) | (group == 3)
    lower = group < 2
    even = (group & 1) == 0

    def pool(v):
        a = jnp.where(outer, v[0], v[2]) + pltpu.roll(jnp.where(outer, v[2], v[0]), 64, 1)
        b = jnp.where(lower, v[1], v[3]) + pltpu.roll(jnp.where(lower, v[3], v[1]), 64, 1)
        return jnp.where(even, a, b) + pltpu.roll(jnp.where(even, b, a), 32, 1)

    def run(match):
        def body(step, carry):
            chunk = chunk_of(step)
            start = chunk * row_step
            date_copy(match, chunk).wait_recv()
            if match == 1:
                date_copy(match, chunk).wait_send()

                @pl.when(step + in_flight < chunks)
                def _():
                    date_copy(match, chunk_of(step + in_flight)).start()

            for slot in range(slots):
                place = place_of(partners_ref, match, slot, slots)
                spot = match * slots + slot
                filter_rows(lambda i, q: own_ref[place, start + i, q], spot, 2 * slot)
                filter_rows(lambda i, q: got_ref[match, slot, start + i, q], spot, 2 * slot + 1)
            for slot in range(slots):
                for i in range(row_step):
                    for a in range(tiles // 4):
                        planes = [[], [], [], []]
                        for b in range(4):
                            q = 4 * a + b
                            one = band_ref[2 * slot, i, q].astype(jnp.float32)
                            two = band_ref[2 * slot + 1, i, q].astype(jnp.float32)
                            fr, fi = one[:, :lanes], one[:, lanes:]
                            sr, si = two[:, :lanes], two[:, lanes:]
                            planes[0].append(fr * sr + fi * si)
                            planes[1].append(fi * sr - fr * si)
                            planes[2].append(fr * fr + fi * fi)
                            planes[3].append(sr * sr + si * si)
                        for p in range(4):
                            looks_ref[match, start + i, slot, p, a] = pool(planes[p])

            @pl.when((chunk >= low_first) & can_up)
            def _():
                low_out_ref[match, pl.ds((chunk - low_first) * row_step, row_step)] = looks_ref[
                    match, pl.ds(start, row_step)
                ].astype(jnp.bfloat16)
                low_copy(match, chunk).start()

            @pl.when((chunk <= high_last) & can_down)
            def _():
                high_out_ref[match, pl.ds(start, row_step)] = looks_ref[match, pl.ds(start, row_step)].astype(
                    jnp.bfloat16
                )
                high_copy(match, chunk).start()

            return carry

        return body

    for match in range(2):
        lax.fori_loop(0, chunks, run(match), 0)

    for match in range(2):

        def settle_low(chunk, carry):
            @pl.when(can_up)
            def _():
                low_copy(match, chunk).wait_send()

            @pl.when(can_down)
            def _():
                low_copy(match, chunk).wait_recv()

            return carry

        def settle_high(chunk, carry):
            @pl.when(can_down)
            def _():
                high_copy(match, chunk).wait_send()

            @pl.when(can_up)
            def _():
                high_copy(match, chunk).wait_recv()

            return carry

        lax.fori_loop(low_first, chunks, settle_low, 0)
        lax.fori_loop(0, high_last + 1, settle_high, 0)

    def settle_near(chunk, carry):
        date_copy(0, chunk).wait_send()
        return carry

    lax.fori_loop(0, chunks, settle_near, 0)


def exchange(partners, taps, own):
    slots, rows, tiles = own.shape[:3]
    chunks = rows // row_step
    groups, strips = lax.axis_size("date"), lax.axis_size("strip")
    tail = (slots, 4, tiles // 4, segments, lanes)
    high_rows = ((above - 1) // row_step + 1) * row_step
    in_vmem = pl.BlockSpec(memory_space=pltpu.VMEM)
    semaphores = pltpu.SemaphoreType.DMA((2, chunks))
    return pl.pallas_call(
        lambda *refs: exchange_kernel(groups, strips, *refs),
        out_shape=(
            jax.ShapeDtypeStruct((2, rows) + tail, jnp.float32),
            jax.ShapeDtypeStruct((2, below) + tail, jnp.bfloat16),
            jax.ShapeDtypeStruct((2, high_rows) + tail, jnp.bfloat16),
        ),
        in_specs=[pl.BlockSpec(memory_space=pltpu.SMEM), in_vmem, in_vmem],
        out_specs=[in_vmem] * 3,
        scratch_shapes=[
            pltpu.VMEM((2,) + own.shape, jnp.bfloat16),
            pltpu.VMEM((2 * slots, 2, 2 * lanes, 2 * lanes), jnp.bfloat16),
            pltpu.VMEM((2 * slots, row_step, tiles, segments, 2 * lanes), jnp.bfloat16),
            pltpu.VMEM((2, below) + tail, jnp.bfloat16),
            pltpu.VMEM((2, high_rows) + tail, jnp.bfloat16),
        ]
        + [semaphores] * 6,
        compiler_params=pltpu.CompilerParams(
            vmem_limit_bytes=36 << 20, collective_id=0, has_side_effects=True
        ),
        name="exchange",
    )(partners, taps, own)


def finish_kernel(places_ref, looks_ref, low_ref, high_ref, cross_ref, coherence_ref, turn_ref):
    rows, halves = looks_ref.shape[1], looks_ref.shape[4]
    for a in range(halves):
        for h in range(0, segments, 8):
            window = []
            for p in range(4):
                e = [low_ref[0, i, 0, p, a].astype(jnp.float32)[h : h + 8] for i in range(below)]
                e += [looks_ref[0, i, 0, p, a, h : h + 8, :] for i in range(rows)]
                e += [high_ref[0, i, 0, p, a].astype(jnp.float32)[h : h + 8] for i in range(above)]
                s2 = [e[i] + e[i + 1] for i in range(len(e) - 1)]
                s4 = [s2[i] + s2[i + 2] for i in range(len(s2) - 2)]
                s8 = [s4[i] + s4[i + 4] for i in range(len(s4) - 4)]
                window.append([s8[r] + s8[r + 8] + s4[r + 16] for r in range(rows)])
            for r in range(rows):
                cr, ci, pf, ps = (window[p][r] for p in range(4))
                spot = pl.ds(h * rows + r, 8, stride=rows)
                turn_ref[0, spot, :] = cr / 80.0
                turn_ref[1, spot, :] = ci / 80.0
                turn_ref[2, spot, :] = jnp.sqrt(cr * cr + ci * ci) * lax.rsqrt(pf * ps + epsilon)
        for s in range(segments):
            column = (s * halves + a) * lanes
            for k in range(2):
                cross_ref[0, 0, k, :, column : column + lanes] = turn_ref[
                    k, s * rows : (s + 1) * rows, :
                ].astype(jnp.bfloat16)
            coherence_ref[0, 0, :, column : column + lanes] = turn_ref[
                2, s * rows : (s + 1) * rows, :
            ].astype(jnp.bfloat16)


def finish(places, looks, low, high):
    matches, rows, dates = looks.shape[:3]
    tail = looks.shape[3:]
    columns = tail[1] * segments * lanes
    block = lambda n: pl.BlockSpec((1, n, 1) + tail, lambda m, i, p: (m, 0, i, 0, 0, 0, 0))
    return pl.pallas_call(
        finish_kernel,
        out_shape=(
            jax.ShapeDtypeStruct((matches, dates, 2, rows, columns), jnp.bfloat16),
            jax.ShapeDtypeStruct((matches, dates, rows, columns), jnp.bfloat16),
        ),
        grid_spec=pltpu.PrefetchScalarGridSpec(
            num_scalar_prefetch=1,
            grid=(matches, dates),
            in_specs=[block(rows), block(low.shape[1]), block(high.shape[1])],
            out_specs=[
                pl.BlockSpec((1, 1, 2, rows, columns), lambda m, i, p: (m, place_of(p, m, i, dates), 0, 0, 0)),
                pl.BlockSpec((1, 1, rows, columns), lambda m, i, p: (m, place_of(p, m, i, dates), 0, 0)),
            ],
            scratch_shapes=[pltpu.VMEM((3, segments * rows, lanes), jnp.float32)],
        ),
        compiler_params=pltpu.CompilerParams(vmem_limit_bytes=10 << 20),
        name="finish",
    )(places, looks, low, high)


def arrange(images):
    dates, rows, _, samples = images.shape
    tiles = samples // (segments * lanes)
    images = images.reshape(dates, rows, 2, segments, tiles, lanes)
    images = with_layout_constraint(images, Layout(major_to_minor=(0, 1, 3, 4, 2, 5)))
    return images.transpose(0, 1, 4, 3, 2, 5).reshape(dates, rows, tiles, segments, 2 * lanes)


def per_device(acquisitions, partners, band_shifts):
    dates = acquisitions.shape[0]
    taps = make_taps(band_shifts).reshape(2 * dates, 2, lanes)
    looks, low, high = exchange(partners, taps, arrange(acquisitions))
    return finish(partners, looks, low, high)


def solution(mesh):
    in_specs = (
        P(("grp", "date"), "strip", None, None),
        P(None, ("grp", "date")),
        P(None, ("grp", "date")),
    )
    out_specs = (
        P(None, ("grp", "date"), None, "strip", None),
        P(None, ("grp", "date"), "strip", None),
    )
    return jax.shard_map(
        per_device, mesh=mesh, in_specs=in_specs, out_specs=out_specs, check_vma=False
    )
```

```python
import math

import jax
import jax.numpy as jnp
from jax import lax
from jax.experimental import pallas as pl
from jax.experimental.layout import Layout, with_layout_constraint

from jax.experimental.pallas import tpu as pltpu
from jax.sharding import PartitionSpec as P

band_width = 0.8
bin_count = 256.0
epsilon = 1e-06
below = 10
above = 9
row_step = 2
in_flight = 3
lanes = 128
segments = 16


def make_taps(shift_bins):
    positions = jnp.arange(64, dtype=jnp.float32)
    centred = positions - 31.5
    hamming = 0.54 - 0.46 * jnp.cos(2.0 * math.pi * positions / 63.0)
    lowpass = hamming * band_width * jnp.sinc(band_width * centred)
    angles = 2.0 * math.pi * shift_bins.astype(jnp.float32)[..., None] * centred / bin_count
    taps = jnp.stack([lowpass * jnp.cos(angles), lowpass * jnp.sin(angles)], axis=-2)
    taps = taps.astype(jnp.bfloat16).astype(jnp.float32)
    zeros = jnp.zeros(taps.shape[:-1] + (64,), jnp.float32)
    return jnp.concatenate([taps[..., 32:], zeros, taps[..., :32]], axis=-1)


def circulant(row):
    block = jnp.broadcast_to(row, (32, lanes))
    parts = [pltpu.roll(block, phase, 1, stride=4, stride_axis=0) for phase in range(4)]
    return jnp.concatenate(parts, axis=0).T


def place_of(partners_ref, match, slot, dates):
    place = 0
    for i in range(1, dates):
        place = place + jnp.where(lax.rem(partners_ref[match, i], dates) == slot, i, 0)
    return place


def build_weights(taps_ref, weight_ref, spot, source):
    real_part = circulant(taps_ref[source, 0:1, :])
    imag_part = circulant(taps_ref[source, 1:2, :])
    k = lax.broadcasted_iota(jnp.int32, (lanes, lanes), 0)
    c = lax.broadcasted_iota(jnp.int32, (lanes, lanes), 1)
    t = 4 * (c & 31) + (c >> 5)
    inside = jnp.abs(k - t) < 64
    for place, mask in ((0, inside), (1, jnp.logical_not(inside))):
        re = jnp.where(mask, real_part, 0.0)
        im = jnp.where(mask, imag_part, 0.0)
        weight_ref[spot, place, 0:lanes, 0:lanes] = re.astype(jnp.bfloat16)
        weight_ref[spot, place, 0:lanes, lanes:] = im.astype(jnp.bfloat16)
        weight_ref[spot, place, lanes:, 0:lanes] = (-im).astype(jnp.bfloat16)
        weight_ref[spot, place, lanes:, lanes:] = re.astype(jnp.bfloat16)


def exchange_kernel(
    groups, strips, partners_ref, taps_ref, own_ref, looks_ref, low_ref, high_ref, made_ref,
    turn_ref, got_ref, weight_ref, band_ref, low_out_ref, high_out_ref,
    got_send, got_recv, low_send, low_recv, high_send, high_recv,
):
    slots, rows, tiles = own_ref.shape[:3]
    chunks = rows // row_step
    low_first = (rows - below) // row_step
    high_last = (above - 1) // row_step
    me = lax.axis_index("date")
    strip = lax.axis_index("strip")
    peers = (me + 1 - 2 * lax.rem(me, 2), lax.rem(me + groups // 2, groups))
    can_up = strip < strips - 1
    can_down = strip > 0

    barrier = pltpu.get_barrier_semaphore()
    for peer in peers:
        pl.semaphore_signal(barrier, inc=1, device_id={"date": peer}, device_id_type=pl.DeviceIdType.MESH)

    @pl.when(can_up)
    def _():
        pl.semaphore_signal(barrier, inc=1, device_id={"strip": strip + 1}, device_id_type=pl.DeviceIdType.MESH)

    @pl.when(can_down)
    def _():
        pl.semaphore_signal(barrier, inc=1, device_id={"strip": strip - 1}, device_id_type=pl.DeviceIdType.MESH)

    pl.semaphore_wait(barrier, 2 + can_up.astype(jnp.int32) + can_down.astype(jnp.int32))

    def chunk_of(step):
        half = step // (chunks // 2)
        return (chunks - 1 - step) * (1 - half) + (step - chunks // 2) * half

    def date_copy(match, chunk):
        spot = pl.ds(chunk * row_step, row_step)
        return pltpu.make_async_remote_copy(
            src_ref=own_ref.at[:, spot],
            dst_ref=got_ref.at[match, :, spot],
            send_sem=got_send.at[match, chunk],
            recv_sem=got_recv.at[match, chunk],
            device_id={"date": peers[match]},
            device_id_type=pl.DeviceIdType.MESH,
        )

    def low_copy(match, chunk):
        spot = pl.ds((chunk - low_first) * row_step, row_step)
        return pltpu.make_async_remote_copy(
            src_ref=low_out_ref.at[match, spot],
            dst_ref=low_ref.at[match, spot],
            send_sem=low_send.at[match, chunk],
            recv_sem=low_recv.at[match, chunk],
            device_id={"strip": strip + 1},
            device_id_type=pl.DeviceIdType.MESH,
        )

    def high_copy(match, chunk):
        spot = pl.ds(chunk * row_step, row_step)
        return pltpu.make_async_remote_copy(
            src_ref=high_out_ref.at[match, spot],
            dst_ref=high_ref.at[match, spot],
            send_sem=high_send.at[match, chunk],
            recv_sem=high_recv.at[match, chunk],
            device_id={"strip": strip - 1},
            device_id_type=pl.DeviceIdType.MESH,
        )

    def start_dates(match):
        def body(step, carry):
            date_copy(match, chunk_of(step)).start()
            return carry

        return body

    lax.fori_loop(0, in_flight, start_dates(1), 0)
    lax.fori_loop(0, chunks, start_dates(0), 0)

    @pl.when(strip == 0)
    def _():
        low_ref[...] = jnp.zeros(low_ref.shape, low_ref.dtype)

    @pl.when(strip == strips - 1)
    def _():
        high_ref[...] = jnp.zeros(high_ref.shape, high_ref.dtype)

    def weigh(spot, carry):
        match = spot // slots
        place = place_of(partners_ref, match, lax.rem(spot, slots), slots)
        build_weights(taps_ref, weight_ref, spot, match * slots + place)
        return carry

    lax.fori_loop(0, 2 * slots, weigh, 0)

    lane = lax.broadcasted_iota(jnp.int32, (segments, 2 * lanes), 1) & (lanes - 1)
    segment = lax.broadcasted_iota(jnp.int32, (segments, 2 * lanes), 0)
    from_before = jnp.where(lane >= 64, 1.0, 0.0).astype(jnp.bfloat16)
    from_after = jnp.where(lane < 64, 1.0, 0.0).astype(jnp.bfloat16)

    def filter_rows(load, spot, band):
        current, edges = [], []
        for i in range(row_step):
            x = [load(i, q) for q in range(tiles)]
            head = pltpu.roll(x[-1].astype(jnp.float32), 1, 0)
            head = jnp.where(segment == 0, 0.0, head).astype(jnp.bfloat16)
            tail = pltpu.roll(x[0].astype(jnp.float32), segments - 1, 0)
            tail = jnp.where(segment == segments - 1, 0.0, tail).astype(jnp.bfloat16)
            y = [head] + x + [tail]
            current += x
            edges += [y[q] * from_before + y[q + 2] * from_after for q in range(tiles)]
        current = jnp.concatenate(current, axis=0)
        edges = jnp.concatenate(edges, axis=0)
        out = jnp.dot(current, weight_ref[spot, 0], preferred_element_type=jnp.float32)
        out = out + jnp.dot(edges, weight_ref[spot, 1], preferred_element_type=jnp.float32)
        band_ref[band] = out.astype(jnp.bfloat16).reshape(row_step, tiles, segments, 2 * lanes)

    group = lax.broadcasted_iota(jnp.int32, (segments, lanes), 1) >> 5
    outer = (group == 0) | (group == 3)
    lower = group < 2
    even = (group & 1) == 0

    def pool(v):
        a = jnp.where(outer, v[0], v[2]) + pltpu.roll(jnp.where(outer, v[2], v[0]), 64, 1)
        b = jnp.where(lower, v[1], v[3]) + pltpu.roll(jnp.where(lower, v[3], v[1]), 64, 1)
        return jnp.where(even, a, b) + pltpu.roll(jnp.where(even, b, a), 32, 1)

    def run(match):
        def body(step, carry):
            chunk = chunk_of(step)
            start = chunk * row_step
            date_copy(match, chunk).wait_recv()
            if match == 1:
                date_copy(match, chunk).wait_send()

                @pl.when(step + in_flight < chunks)
                def _():
                    date_copy(match, chunk_of(step + in_flight)).start()

            for slot in range(slots):
                place = place_of(partners_ref, match, slot, slots)
                spot = match * slots + slot
                filter_rows(lambda i, q: own_ref[place, start + i, q], spot, 2 * slot)
                filter_rows(lambda i, q: got_ref[match, slot, start + i, q], spot, 2 * slot + 1)
            for slot in range(slots):
                for i in range(row_step):
                    for a in range(tiles // 4):
                        planes = [[], [], [], []]
                        for b in range(4):
                            q = 4 * a + b
                            one = band_ref[2 * slot, i, q].astype(jnp.float32)
                            two = band_ref[2 * slot + 1, i, q].astype(jnp.float32)
                            fr, fi = one[:, :lanes], one[:, lanes:]
                            sr, si = two[:, :lanes], two[:, lanes:]
                            planes[0].append(fr * sr + fi * si)
                            planes[1].append(fi * sr - fr * si)
                            planes[2].append(fr * fr + fi * fi)
                            planes[3].append(sr * sr + si * si)
                        for p in range(4):
                            looks_ref[match, start + i, slot, p, a] = pool(planes[p])

            @pl.when((chunk >= low_first) & can_up)
            def _():
                low_out_ref[match, pl.ds((chunk - low_first) * row_step, row_step)] = looks_ref[
                    match, pl.ds(start, row_step)
                ].astype(jnp.bfloat16)
                low_copy(match, chunk).start()

            @pl.when((chunk <= high_last) & can_down)
            def _():
                high_out_ref[match, pl.ds(start, row_step)] = looks_ref[match, pl.ds(start, row_step)].astype(
                    jnp.bfloat16
                )
                high_copy(match, chunk).start()

            return carry

        return body

    def settle(match):
        def settle_low(chunk, carry):
            @pl.when(can_up)
            def _():
                low_copy(match, chunk).wait_send()

            @pl.when(can_down)
            def _():
                low_copy(match, chunk).wait_recv()

            return carry

        def settle_high(chunk, carry):
            @pl.when(can_down)
            def _():
                high_copy(match, chunk).wait_send()

            @pl.when(can_up)
            def _():
                high_copy(match, chunk).wait_recv()

            return carry

        lax.fori_loop(low_first, chunks, settle_low, 0)
        lax.fori_loop(0, high_last + 1, settle_high, 0)

    def make_first(slot, carry):
        def store_cross(k, column, value):
            made_ref[slot, k, :, column] = value

        def store_coherence(column, value):
            made_ref[slot, 2, :, column] = value

        window_rows(
            lambda i, p, a: low_ref[0, i, slot, p, a],
            lambda i, p, a, h: looks_ref[0, i, slot, p, a, h : h + 8, :],
            lambda i, p, a: high_ref[0, i, slot, p, a],
            store_cross,
            store_coherence,
            turn_ref,
            rows,
            tiles // 4,
        )
        return carry

    lax.fori_loop(0, chunks, run(0), 0)
    lax.fori_loop(0, chunks - 3, run(1), 0)
    settle(0)
    lax.fori_loop(0, slots, make_first, 0)
    lax.fori_loop(chunks - 3, chunks, run(1), 0)
    settle(1)

    def settle_near(chunk, carry):
        date_copy(0, chunk).wait_send()
        return carry

    lax.fori_loop(0, chunks, settle_near, 0)


def exchange(partners, taps, own):
    slots, rows, tiles = own.shape[:3]
    chunks = rows // row_step
    groups, strips = lax.axis_size("date"), lax.axis_size("strip")
    tail = (slots, 4, tiles // 4, segments, lanes)
    high_rows = ((above - 1) // row_step + 1) * row_step
    in_vmem = pl.BlockSpec(memory_space=pltpu.VMEM)
    semaphores = pltpu.SemaphoreType.DMA((2, chunks))
    return pl.pallas_call(
        lambda *refs: exchange_kernel(groups, strips, *refs),
        out_shape=(
            jax.ShapeDtypeStruct((2, rows) + tail, jnp.float32),
            jax.ShapeDtypeStruct((2, below) + tail, jnp.bfloat16),
            jax.ShapeDtypeStruct((2, high_rows) + tail, jnp.bfloat16),
            jax.ShapeDtypeStruct((slots, 3, rows, tail[2] * segments * lanes), jnp.bfloat16),
        ),
        in_specs=[pl.BlockSpec(memory_space=pltpu.SMEM), in_vmem, in_vmem],
        out_specs=[in_vmem] * 4,
        scratch_shapes=[
            pltpu.VMEM((3, segments * rows, lanes), jnp.float32),
            pltpu.VMEM((2,) + own.shape, jnp.bfloat16),
            pltpu.VMEM((2 * slots, 2, 2 * lanes, 2 * lanes), jnp.bfloat16),
            pltpu.VMEM((2 * slots, row_step, tiles, segments, 2 * lanes), jnp.bfloat16),
            pltpu.VMEM((2, below) + tail, jnp.bfloat16),
            pltpu.VMEM((2, high_rows) + tail, jnp.bfloat16),
        ]
        + [semaphores] * 6,
        compiler_params=pltpu.CompilerParams(
            vmem_limit_bytes=36 << 20, collective_id=0, has_side_effects=True
        ),
        name="exchange",
    )(partners, taps, own)


def window_rows(load_low, load_looks, load_high, store_cross, store_coherence, turn_ref, rows, halves):
    for a in range(halves):
        for h in range(0, segments, 8):
            window = []
            for p in range(4):
                e = [load_low(i, p, a).astype(jnp.float32)[h : h + 8] for i in range(below)]
                e += [load_looks(i, p, a, h) for i in range(rows)]
                e += [load_high(i, p, a).astype(jnp.float32)[h : h + 8] for i in range(above)]
                s2 = [e[i] + e[i + 1] for i in range(len(e) - 1)]
                s4 = [s2[i] + s2[i + 2] for i in range(len(s2) - 2)]
                s8 = [s4[i] + s4[i + 4] for i in range(len(s4) - 4)]
                window.append([s8[r] + s8[r + 8] + s4[r + 16] for r in range(rows)])
            for r in range(rows):
                cr, ci, pf, ps = (window[p][r] for p in range(4))
                spot = pl.ds(h * rows + r, 8, stride=rows)
                turn_ref[0, spot, :] = cr / 80.0
                turn_ref[1, spot, :] = ci / 80.0
                turn_ref[2, spot, :] = jnp.sqrt(cr * cr + ci * ci) * lax.rsqrt(pf * ps + epsilon)
        for s in range(segments):
            column = slice((s * halves + a) * lanes, (s * halves + a + 1) * lanes)
            for k in range(2):
                store_cross(k, column, turn_ref[k, s * rows : (s + 1) * rows, :].astype(jnp.bfloat16))
            store_coherence(column, turn_ref[2, s * rows : (s + 1) * rows, :].astype(jnp.bfloat16))


def finish_kernel(places_ref, looks_ref, low_ref, high_ref, made_ref, cross_ref, coherence_ref, turn_ref):
    rows, halves = looks_ref.shape[1], looks_ref.shape[4]

    @pl.when(pl.program_id(0) == 0)
    def _():
        cross_ref[0, 0] = made_ref[0, 0:2]
        coherence_ref[0, 0] = made_ref[0, 2]

    @pl.when(pl.program_id(0) == 1)
    def _():
        def store_cross(k, column, value):
            cross_ref[0, 0, k, :, column] = value

        def store_coherence(column, value):
            coherence_ref[0, 0, :, column] = value

        window_rows(
            lambda i, p, a: low_ref[0, i, 0, p, a],
            lambda i, p, a, h: looks_ref[0, i, 0, p, a, h : h + 8, :],
            lambda i, p, a: high_ref[0, i, 0, p, a],
            store_cross,
            store_coherence,
            turn_ref,
            rows,
            halves,
        )


def finish(places, looks, low, high, made):
    matches, rows, dates = looks.shape[:3]
    tail = looks.shape[3:]
    columns = tail[1] * segments * lanes
    block = lambda n: pl.BlockSpec((1, n, 1) + tail, lambda m, i, p: (1, 0, i * m, 0, 0, 0, 0))
    return pl.pallas_call(
        finish_kernel,
        out_shape=(
            jax.ShapeDtypeStruct((matches, dates, 2, rows, columns), jnp.bfloat16),
            jax.ShapeDtypeStruct((matches, dates, rows, columns), jnp.bfloat16),
        ),
        grid_spec=pltpu.PrefetchScalarGridSpec(
            num_scalar_prefetch=1,
            grid=(matches, dates),
            in_specs=[block(rows), block(low.shape[1]), block(high.shape[1]),
                pl.BlockSpec((1, 3, rows, columns), lambda m, i, p: (i * (1 - m) + (dates - 1) * m, 0, 0, 0))],
            out_specs=[
                pl.BlockSpec((1, 1, 2, rows, columns), lambda m, i, p: (m, place_of(p, m, i, dates), 0, 0, 0)),
                pl.BlockSpec((1, 1, rows, columns), lambda m, i, p: (m, place_of(p, m, i, dates), 0, 0)),
            ],
            scratch_shapes=[pltpu.VMEM((3, segments * rows, lanes), jnp.float32)],
        ),
        compiler_params=pltpu.CompilerParams(vmem_limit_bytes=10 << 20),
        name="finish",
    )(places, looks, low, high, made)


def arrange(images):
    dates, rows, _, samples = images.shape
    tiles = samples // (segments * lanes)
    images = images.reshape(dates, rows, 2, segments, tiles, lanes)
    images = with_layout_constraint(images, Layout(major_to_minor=(0, 1, 3, 4, 2, 5)))
    return images.transpose(0, 1, 4, 3, 2, 5).reshape(dates, rows, tiles, segments, 2 * lanes)


def per_device(acquisitions, partners, band_shifts):
    dates = acquisitions.shape[0]
    taps = make_taps(band_shifts).reshape(2 * dates, 2, lanes)
    looks, low, high, made = exchange(partners, taps, arrange(acquisitions))
    return finish(partners, looks, low, high, made)


def solution(mesh):
    in_specs = (
        P(("grp", "date"), "strip", None, None),
        P(None, ("grp", "date")),
        P(None, ("grp", "date")),
    )
    out_specs = (
        P(None, ("grp", "date"), None, "strip", None),
        P(None, ("grp", "date"), "strip", None),
    )
    return jax.shard_map(
        per_device, mesh=mesh, in_specs=in_specs, out_specs=out_specs, check_vma=False
    )
```
